256 devices in a mesh: blk: 8 (over x_hi, y), grp: 32 (over z, x_lo, core).
Axes of the slice: x: 4 (x_hi: 2, x_lo: 2; x = x_hi * 2 + x_lo), y: 4, z: 8, core: 2. Of those that a mesh axis runs over, the one named last changes fastest.
Arguments:
- amplitudes: bfloat16 [4, 4096, 1024], P(None, 'blk'), may hold values from -6 to 6
- pair_screen: int32 [4, 256], P(None, 'blk'), may hold values 0 or 1
- integrals: bfloat16 [256, 1024, 1024], P(('blk', 'grp')), may hold values from -0.1875 to 0.1875
- tile_ab: int32 [8, 32], replicated, may hold values from 0 to 49, as said below
- tile_cd: int32 [8, 32], replicated, may hold values from 0 to 3
- residual_in: float32 [4096, 50, 1024], P(('blk', 'grp')), may hold values from -6 to 6
Outputs:
- residual: float32 [4096, 50, 1024], P(('blk', 'grp'))
The draws below stay inside these ranges and needn't reach their ends.
Inputs may be any that keep to these rules, and one draw needn't show every extreme that they name: `tile_ab`: the 8 integral tiles that share a column g name 2 to 4 distinct b tiles, and in every draw some column names exactly 4.
All inputs are finite; a program needn't handle non-finite values. No bound on the sum of `pair_screen` on one device may be relied on, other than what follows from the above.
Results may differ from the reference program's by a relative error of at most 0.0003.
Values may be sent and summed in bfloat16 or wider, within the bound.
A program may use at most 128 MiB of HBM per device.

```python
import jax
import jax.numpy as jnp
from jax import lax

NCD = 4
PBR = 16
UNIQ = 4
NAB = 50
K = 1024
PAIRS = 4096
NT = 256
N_BLK = 8
N_GRP = 32


def draw_tile_ab(key, part):
    key_count, key_widest, key_cands, key_picks, key_order = jax.random.split(key, 5)
    counts = jax.random.randint(key_count, (N_GRP,), 2, UNIQ + 1)
    widest = jax.random.randint(key_widest, (), 0, N_GRP)
    counts = jnp.where(jnp.arange(N_GRP) == widest, UNIQ, counts)
    cand_keys = jax.random.split(key_cands, N_GRP)
    candidates = jax.vmap(lambda single: jax.random.permutation(single, NAB)[:UNIQ])(cand_keys)
    picks = jax.random.randint(key_picks, (N_BLK, N_GRP), 0, 1 << 20) % counts[None, :]
    ranks = jnp.arange(N_BLK)[:, None]
    picks = jnp.where(ranks < counts[None, :], ranks, picks)
    order_keys = jax.random.split(key_order, N_GRP)
    orders = jax.vmap(lambda single: jax.random.permutation(single, N_BLK))(order_keys)
    picks = jnp.take_along_axis(picks, orders.T, axis=0)
    chosen = jnp.take_along_axis(candidates.T, picks, axis=0)
    return chosen.astype(jnp.int32)


def plant(drawn, own_key, smallest, largest):
    longest = drawn.shape.index(max(drawn.shape))
    spots = []
    for shift in (0, 1):
        where = [jax.random.randint(jax.random.fold_in(own_key, axis), (), 0, length) for axis, length in enumerate(drawn.shape)]
        where[longest] = (where[longest] + shift) % drawn.shape[longest]
        spots.append(tuple(where))
    return drawn.at[spots[0]].set(smallest).at[spots[1]].set(largest)


def block_scale(key, extent, cuts, smallest, largest):
    def one(dim, parts):
        heights = jax.random.uniform(jax.random.fold_in(jax.random.fold_in(key, 6), dim), (parts,), jnp.float32, smallest / len(cuts), largest / len(cuts))
        return jnp.repeat(jnp.exp(heights), extent[dim] // parts).reshape((-1,) + (1,) * (len(extent) - dim - 1))

    factor_of = one(*cuts[0])
    for cut in cuts[1:]:
        factor_of = factor_of * one(*cut)
    return factor_of


def normal_values(stream_key, extent, scale, reach, cuts=(), kind=jnp.bfloat16):
    drawn = jax.random.normal(stream_key, extent, jnp.float32) * scale
    if len(cuts) > 0:
        drawn = block_scale(stream_key, extent, cuts, -0.22, 0.18) * drawn
    return jnp.clip(drawn, min=-reach, max=reach).astype(kind)


def setup_inputs(seed: int = 0) -> dict:
    seeds = jax.random.split(jax.random.key(seed), 7)
    amplitudes = normal_values(seeds[0], (NCD, PAIRS, K), 1.0, 6.0, ((1, 8),))
    pair_screen = plant((jax.random.randint(seeds[1], (NCD, PAIRS // PBR), 0, 4) < 3).astype(jnp.int32), jax.random.fold_in(seeds[1], 1), 0, 1)
    integrals = normal_values(seeds[2], (NT, K, K), K ** -0.5, 0.1875, ((0, 256),))
    tile_ab = draw_tile_ab(jax.random.fold_in(seeds[6], 71), 0)
    tile_cd = plant(jax.random.randint(seeds[4], (N_BLK, N_GRP), 0, NCD), jax.random.fold_in(seeds[4], 1), 0, NCD - 1).astype(jnp.int32)
    residual_in = normal_values(seeds[5], (PAIRS, NAB, K), 1.0, 6.0, ((0, 256),), jnp.float32)
    return {"amplitudes": amplitudes, "pair_screen": pair_screen, "integrals": integrals, "tile_ab": tile_ab, "tile_cd": tile_cd, "residual_in": residual_in}


def reference(amplitudes, pair_screen, integrals, tile_ab, tile_cd, residual_in):
    row_mask = jnp.repeat(pair_screen, PBR, axis=1).astype(jnp.bfloat16)
    masked = amplitudes * row_mask[:, :, None]
    flat_ab = tile_ab.reshape(-1).astype(jnp.int32)
    flat_cd = tile_cd.reshape(-1).astype(jnp.int32)

    def add_tile(position, running):
        position = jnp.asarray(position).astype(jnp.int32)
        cd_index = flat_cd[position].astype(jnp.int32)
        ab_index = flat_ab[position].astype(jnp.int32)
        rows_in = lax.dynamic_index_in_dim(masked, cd_index, 0, keepdims=False)
        panel = lax.dynamic_index_in_dim(integrals, position, 0, keepdims=False)
        product = jnp.dot(rows_in, panel, preferred_element_type=jnp.float32)
        earlier = lax.dynamic_index_in_dim(running, ab_index, 1, keepdims=False)
        return lax.dynamic_update_index_in_dim(running, earlier + product, ab_index, 1)

    return lax.fori_loop(0, NT, add_tile, residual_in)
```

```python
import jax
import jax.numpy as jnp
from jax import lax
from jax.sharding import PartitionSpec as P

SLOTS = 4


def slot_of(column_ab):
    tiles = column_ab.shape[0]
    order = jnp.arange(tiles).reshape((tiles,) + (1,) * (column_ab.ndim - 1))
    same = column_ab[:, None] == column_ab[None, :]
    first = jnp.argmax(same, axis=1)
    is_first = first == order
    earlier = order[None, :] < first[:, None]
    return jnp.sum(earlier & is_first[None, :], axis=1).astype(jnp.int32)


def shards(amplitudes, pair_screen, integrals, tile_ab, tile_cd, residual_in):
    grp_count = lax.axis_size("grp")
    grp_position = lax.axis_index("grp")
    owner_rows, ab_tiles, tile_width = residual_in.shape
    group_rows = amplitudes.shape[1]
    row_mask = jnp.repeat(pair_screen, owner_rows, axis=1).astype(jnp.bfloat16)
    masked = amplitudes * row_mask[:, :, None]
    column_cd = lax.dynamic_index_in_dim(tile_cd, grp_position, 1, keepdims=False)
    column_ab = lax.dynamic_index_in_dim(tile_ab, grp_position, 1, keepdims=False)
    column_slot = slot_of(column_ab)
    portion = lax.all_gather(integrals, "blk", axis=0, tiled=True)
    running = jnp.zeros((SLOTS, group_rows, tile_width), jnp.float32)
    for offset in range(portion.shape[0]):
        rows_in = lax.dynamic_index_in_dim(masked, column_cd[offset], 0, keepdims=False)
        product = jnp.dot(rows_in, portion[offset], preferred_element_type=jnp.float32)
        slot = column_slot[offset]
        earlier = lax.dynamic_index_in_dim(running, slot, 0, keepdims=False)
        running = lax.dynamic_update_index_in_dim(running, earlier + product, slot, 0)
    arrived = lax.all_to_all(
        running.reshape(SLOTS, grp_count, owner_rows, tile_width),
        "grp",
        split_axis=1,
        concat_axis=1,
        tiled=True,
    )
    all_slot = slot_of(tile_ab)
    slot_hit = all_slot[:, None, :] == jnp.arange(SLOTS)[None, :, None]
    ab_hit = tile_ab[None, :, :] == jnp.arange(ab_tiles)[:, None, None]
    onehot = jnp.any(ab_hit[:, :, None, :] & slot_hit[None, :, :, :], axis=1).astype(jnp.float32)
    summed = jnp.einsum(
        "nsg,sgrc->rnc", onehot, arrived, precision=lax.Precision.HIGHEST, preferred_element_type=jnp.float32
    )
    return residual_in + summed


def solution(mesh):
    in_specs = (
        P(None, "blk", None),
        P(None, "blk"),
        P(("blk", "grp"), None, None),
        P(),
        P(),
        P(("blk", "grp"), None, None),
    )
    out_specs = P(("blk", "grp"), None, None)
    return jax.shard_map(shards, mesh=mesh, in_specs=in_specs, out_specs=out_specs, check_vma=False)
```

```python
import jax
import jax.numpy as jnp
from jax import lax
from jax.sharding import PartitionSpec as P

SLOTS = 4
CHUNKS = 4


def slot_of(column_ab):
    tiles = column_ab.shape[0]
    order = jnp.arange(tiles).reshape((tiles,) + (1,) * (column_ab.ndim - 1))
    same = column_ab[:, None] == column_ab[None, :]
    first = jnp.argmax(same, axis=1)
    is_first = first == order
    earlier = order[None, :] < first[:, None]
    return jnp.sum(earlier & is_first[None, :], axis=1).astype(jnp.int32)


def shards(amplitudes, pair_screen, integrals, tile_ab, tile_cd, residual_in):
    grp_count = lax.axis_size("grp")
    grp_position = lax.axis_index("grp")
    owner_rows, ab_tiles, tile_width = residual_in.shape
    group_rows = amplitudes.shape[1]
    row_mask = jnp.repeat(pair_screen, owner_rows, axis=1).astype(jnp.bfloat16)
    masked = amplitudes * row_mask[:, :, None]
    column_cd = lax.dynamic_index_in_dim(tile_cd, grp_position, 1, keepdims=False)
    column_ab = lax.dynamic_index_in_dim(tile_ab, grp_position, 1, keepdims=False)
    column_slot = slot_of(column_ab)
    all_slot = slot_of(tile_ab)
    slot_hit = all_slot[:, None, :] == jnp.arange(SLOTS)[None, :, None]
    ab_hit = tile_ab[None, :, :] == jnp.arange(ab_tiles)[:, None, None]
    onehot = jnp.any(ab_hit[:, :, None, :] & slot_hit[None, :, :, :], axis=1).astype(jnp.float32)
    chunk = tile_width // CHUNKS
    pieces = []
    for part in range(CHUNKS):
        columns = slice(part * chunk, (part + 1) * chunk)
        portion = lax.all_gather(integrals[:, :, columns], "blk", axis=0, tiled=True)
        running = jnp.zeros((SLOTS, group_rows, chunk), jnp.float32)
        for offset in range(portion.shape[0]):
            rows_in = lax.dynamic_index_in_dim(masked, column_cd[offset], 0, keepdims=False)
            product = jnp.dot(rows_in, portion[offset], preferred_element_type=jnp.float32)
            slot = column_slot[offset]
            earlier = lax.dynamic_index_in_dim(running, slot, 0, keepdims=False)
            running = lax.dynamic_update_index_in_dim(running, earlier + product, slot, 0)
        arrived = lax.all_to_all(
            running.reshape(SLOTS, grp_count, owner_rows, chunk),
            "grp",
            split_axis=1,
            concat_axis=1,
            tiled=True,
        )
        pieces.append(
            jnp.einsum(
                "nsg,sgrc->rnc", onehot, arrived, precision=lax.Precision.HIGHEST, preferred_element_type=jnp.float32
            )
        )
    summed = jnp.concatenate(pieces, axis=2)
    return residual_in + summed


def solution(mesh):
    in_specs = (
        P(None, "blk", None),
        P(None, "blk"),
        P(("blk", "grp"), None, None),
        P(),
        P(),
        P(("blk", "grp"), None, None),
    )
    out_specs = P(("blk", "grp"), None, None)
    return jax.shard_map(shards, mesh=mesh, in_specs=in_specs, out_specs=out_specs, check_vma=False)
```

```python
import jax
import jax.numpy as jnp
from jax import lax
from jax.sharding import PartitionSpec as P

SLOTS = 4
CHUNKS = 4


def slot_of(column_ab):
    tiles = column_ab.shape[0]
    order = jnp.arange(tiles).reshape((tiles,) + (1,) * (column_ab.ndim - 1))
    same = column_ab[:, None] == column_ab[None, :]
    first = jnp.argmax(same, axis=1)
    is_first = first == order
    earlier = order[None, :] < first[:, None]
    return jnp.sum(earlier & is_first[None, :], axis=1).astype(jnp.int32)


def shards(amplitudes, pair_screen, integrals, tile_ab, tile_cd, residual_in):
    grp_count = lax.axis_size("grp")
    grp_position = lax.axis_index("grp")
    owner_rows, ab_tiles, tile_width = residual_in.shape
    group_rows = amplitudes.shape[1]
    row_mask = jnp.repeat(pair_screen, owner_rows, axis=1).astype(jnp.bfloat16)
    masked = amplitudes * row_mask[:, :, None]
    column_cd = lax.dynamic_index_in_dim(tile_cd, grp_position, 1, keepdims=False)
    column_ab = lax.dynamic_index_in_dim(tile_ab, grp_position, 1, keepdims=False)
    column_slot = slot_of(column_ab)
    all_slot = slot_of(tile_ab)
    slot_hit = all_slot[:, None, :] == jnp.arange(SLOTS)[None, :, None]
    ab_hit = tile_ab[None, :, :] == jnp.arange(ab_tiles)[:, None, None]
    onehot = jnp.any(ab_hit[:, :, None, :] & slot_hit[None, :, :, :], axis=1).astype(jnp.float32)
    chunk = tile_width // CHUNKS
    chunked = jnp.transpose(integrals.reshape(integrals.shape[1], CHUNKS, chunk), (1, 0, 2))
    pieces = []
    for part in range(CHUNKS):
        portion = lax.all_gather(chunked[part : part + 1], "blk", axis=0, tiled=True)
        running = jnp.zeros((SLOTS, group_rows, chunk), jnp.float32)
        for offset in range(portion.shape[0]):
            rows_in = lax.dynamic_index_in_dim(masked, column_cd[offset], 0, keepdims=False)
            product = jnp.dot(rows_in, portion[offset], preferred_element_type=jnp.float32)
            slot = column_slot[offset]
            earlier = lax.dynamic_index_in_dim(running, slot, 0, keepdims=False)
            running = lax.dynamic_update_index_in_dim(running, earlier + product, slot, 0)
        arrived = lax.all_to_all(
            running.reshape(SLOTS, grp_count, owner_rows, chunk),
            "grp",
            split_axis=1,
            concat_axis=1,
            tiled=True,
        )
        pieces.append(
            jnp.einsum(
                "nsg,sgrc->rnc", onehot, arrived, precision=lax.Precision.HIGHEST, preferred_element_type=jnp.float32
            )
        )
    summed = jnp.concatenate(pieces, axis=2)
    return residual_in + summed


def solution(mesh):
    in_specs = (
        P(None, "blk", None),
        P(None, "blk"),
        P(("blk", "grp"), None, None),
        P(),
        P(),
        P(("blk", "grp"), None, None),
    )
    out_specs = P(("blk", "grp"), None, None)
    return jax.shard_map(shards, mesh=mesh, in_specs=in_specs, out_specs=out_specs, check_vma=False)
```

```python
import functools

import jax
import jax.numpy as jnp
from jax import lax
from jax.experimental import pallas as pl
from jax.experimental.pallas import tpu as pltpu
from jax.sharding import PartitionSpec as P

SLOTS = 4
CHUNKS = 4


def slot_of(column_ab):
    tiles = column_ab.shape[0]
    order = jnp.arange(tiles).reshape((tiles,) + (1,) * (column_ab.ndim - 1))
    same = column_ab[:, None] == column_ab[None, :]
    first = jnp.argmax(same, axis=1)
    is_first = first == order
    earlier = order[None, :] < first[:, None]
    return jnp.sum(earlier & is_first[None, :], axis=1).astype(jnp.int32)


def gather_kernel(count, source, gathered, send_sems, recv_sems, local_sem):
    me = lax.axis_index("blk")
    column = lax.axis_index("grp")
    local = pltpu.make_async_copy(source, gathered.at[me], local_sem)
    local.start()
    outgoing = []
    for step in range(1, count):
        peer = lax.rem(me + step, count)
        copy = pltpu.make_async_remote_copy(
            src_ref=source,
            dst_ref=gathered.at[me],
            send_sem=send_sems.at[step],
            recv_sem=recv_sems.at[step],
            device_id=(peer, column),
            device_id_type=pl.DeviceIdType.MESH,
        )
        copy.start()
        outgoing.append(copy)
    for step in range(1, count):
        sender = lax.rem(me + count - step, count)
        incoming = pltpu.make_async_remote_copy(
            src_ref=source,
            dst_ref=gathered.at[sender],
            send_sem=send_sems.at[step],
            recv_sem=recv_sems.at[step],
            device_id=(sender, column),
            device_id_type=pl.DeviceIdType.MESH,
        )
        incoming.wait_recv()
    for copy in outgoing:
        copy.wait_send()
    local.wait()


def gather_blk(piece):
    count = lax.axis_size("blk")
    rows, width = piece.shape
    return pl.pallas_call(
        functools.partial(gather_kernel, count),
        out_shape=jax.ShapeDtypeStruct((count, rows, width), piece.dtype),
        in_specs=[pl.BlockSpec(memory_space=pl.ANY)],
        out_specs=pl.BlockSpec(memory_space=pl.ANY),
        scratch_shapes=[
            pltpu.SemaphoreType.DMA((count,)),
            pltpu.SemaphoreType.DMA((count,)),
            pltpu.SemaphoreType.DMA(()),
        ],
        compiler_params=pltpu.CompilerParams(has_side_effects=True),
        cost_estimate=pl.CostEstimate(flops=0, bytes_accessed=2 * count * rows * width * 2, transcendentals=0),
    )(piece)


def shards(amplitudes, pair_screen, integrals, tile_ab, tile_cd, residual_in):
    grp_count = lax.axis_size("grp")
    grp_position = lax.axis_index("grp")
    owner_rows, ab_tiles, tile_width = residual_in.shape
    group_rows = amplitudes.shape[1]
    row_mask = jnp.repeat(pair_screen, owner_rows, axis=1).astype(jnp.bfloat16)
    masked = amplitudes * row_mask[:, :, None]
    column_cd = lax.dynamic_index_in_dim(tile_cd, grp_position, 1, keepdims=False)
    column_ab = lax.dynamic_index_in_dim(tile_ab, grp_position, 1, keepdims=False)
    column_slot = slot_of(column_ab)
    all_slot = slot_of(tile_ab)
    slot_hit = all_slot[:, None, :] == jnp.arange(SLOTS)[None, :, None]
    ab_hit = tile_ab[None, :, :] == jnp.arange(ab_tiles)[:, None, None]
    onehot = jnp.any(ab_hit[:, :, None, :] & slot_hit[None, :, :, :], axis=1).astype(jnp.float32)
    chunk = tile_width // CHUNKS
    chunked = jnp.transpose(integrals.reshape(integrals.shape[1], CHUNKS, chunk), (1, 0, 2))
    pieces = []
    for part in range(CHUNKS):
        portion = gather_blk(chunked[part])
        running = jnp.zeros((SLOTS, group_rows, chunk), jnp.float32)
        for offset in range(portion.shape[0]):
            rows_in = lax.dynamic_index_in_dim(masked, column_cd[offset], 0, keepdims=False)
            product = jnp.dot(rows_in, portion[offset], preferred_element_type=jnp.float32)
            slot = column_slot[offset]
            earlier = lax.dynamic_index_in_dim(running, slot, 0, keepdims=False)
            running = lax.dynamic_update_index_in_dim(running, earlier + product, slot, 0)
        arrived = lax.all_to_all(
            running.reshape(SLOTS, grp_count, owner_rows, chunk),
            "grp",
            split_axis=1,
            concat_axis=1,
            tiled=True,
        )
        pieces.append(
            jnp.einsum(
                "nsg,sgrc->rnc", onehot, arrived, precision=lax.Precision.HIGHEST, preferred_element_type=jnp.float32
            )
        )
    summed = jnp.concatenate(pieces, axis=2)
    return residual_in + summed


def solution(mesh):
    in_specs = (
        P(None, "blk", None),
        P(None, "blk"),
        P(("blk", "grp"), None, None),
        P(),
        P(),
        P(("blk", "grp"), None, None),
    )
    out_specs = P(("blk", "grp"), None, None)
    return jax.shard_map(shards, mesh=mesh, in_specs=in_specs, out_specs=out_specs, check_vma=False)
```

```python
import functools

import jax
import jax.numpy as jnp
from jax import lax
from jax.experimental import pallas as pl
from jax.experimental.pallas import tpu as pltpu
from jax.sharding import PartitionSpec as P

SLOTS = 4
CHUNKS = 4


def slot_of(column_ab):
    tiles = column_ab.shape[0]
    order = jnp.arange(tiles).reshape((tiles,) + (1,) * (column_ab.ndim - 1))
    same = column_ab[:, None] == column_ab[None, :]
    first = jnp.argmax(same, axis=1)
    is_first = first == order
    earlier = order[None, :] < first[:, None]
    return jnp.sum(earlier & is_first[None, :], axis=1).astype(jnp.int32)


def gather_kernel(count, source, gathered, send_sems, recv_sems, local_sem):
    me = lax.axis_index("blk")
    column = lax.axis_index("grp")
    ring = count // 2
    base = (me // ring) * ring
    partner = lax.rem(me + ring, count)
    local = pltpu.make_async_copy(source, gathered.at[me], local_sem)
    local.start()

    def transfer(origin, target, slot):
        return pltpu.make_async_remote_copy(
            src_ref=source if origin is me else gathered.at[origin],
            dst_ref=gathered.at[origin],
            send_sem=send_sems.at[slot],
            recv_sem=recv_sems.at[origin],
            device_id=(target, column),
            device_id_type=pl.DeviceIdType.MESH,
        )

    peers = [base + lax.rem(me - base + step, ring) for step in range(1, ring)]
    outgoing = [transfer(me, partner, 0)]
    for step, peer in enumerate(peers):
        outgoing.append(transfer(me, peer, 1 + step))
    for copy in outgoing:
        copy.start()
    transfer(partner, partner, 0).wait_recv()
    forwarded = [transfer(partner, peer, ring + step) for step, peer in enumerate(peers)]
    for copy in forwarded:
        copy.start()
    for peer in peers:
        transfer(peer, peer, 0).wait_recv()
        transfer(lax.rem(peer + ring, count), peer, 0).wait_recv()
    for copy in outgoing + forwarded:
        copy.wait_send()
    local.wait()


def gather_blk(piece):
    count = lax.axis_size("blk")
    rows, width = piece.shape
    return pl.pallas_call(
        functools.partial(gather_kernel, count),
        out_shape=jax.ShapeDtypeStruct((count, rows, width), piece.dtype),
        in_specs=[pl.BlockSpec(memory_space=pl.ANY)],
        out_specs=pl.BlockSpec(memory_space=pl.ANY),
        scratch_shapes=[
            pltpu.SemaphoreType.DMA((count,)),
            pltpu.SemaphoreType.DMA((count,)),
            pltpu.SemaphoreType.DMA(()),
        ],
        compiler_params=pltpu.CompilerParams(has_side_effects=True),
        cost_estimate=pl.CostEstimate(flops=0, bytes_accessed=2 * count * rows * width * 2, transcendentals=0),
    )(piece)


def shards(amplitudes, pair_screen, integrals, tile_ab, tile_cd, residual_in):
    grp_count = lax.axis_size("grp")
    grp_position = lax.axis_index("grp")
    owner_rows, ab_tiles, tile_width = residual_in.shape
    group_rows = amplitudes.shape[1]
    row_mask = jnp.repeat(pair_screen, owner_rows, axis=1).astype(jnp.bfloat16)
    masked = amplitudes * row_mask[:, :, None]
    column_cd = lax.dynamic_index_in_dim(tile_cd, grp_position, 1, keepdims=False)
    column_ab = lax.dynamic_index_in_dim(tile_ab, grp_position, 1, keepdims=False)
    column_slot = slot_of(column_ab)
    all_slot = slot_of(tile_ab)
    slot_hit = all_slot[:, None, :] == jnp.arange(SLOTS)[None, :, None]
    ab_hit = tile_ab[None, :, :] == jnp.arange(ab_tiles)[:, None, None]
    onehot = jnp.any(ab_hit[:, :, None, :] & slot_hit[None, :, :, :], axis=1).astype(jnp.float32)
    chunk = tile_width // CHUNKS
    chunked = jnp.transpose(integrals.reshape(integrals.shape[1], CHUNKS, chunk), (1, 0, 2))
    pieces = []
    for part in range(CHUNKS):
        portion = gather_blk(chunked[part])
        running = jnp.zeros((SLOTS, group_rows, chunk), jnp.float32)
        for offset in range(portion.shape[0]):
            rows_in = lax.dynamic_index_in_dim(masked, column_cd[offset], 0, keepdims=False)
            product = jnp.dot(rows_in, portion[offset], preferred_element_type=jnp.float32)
            slot = column_slot[offset]
            earlier = lax.dynamic_index_in_dim(running, slot, 0, keepdims=False)
            running = lax.dynamic_update_index_in_dim(running, earlier + product, slot, 0)
        arrived = lax.all_to_all(
            running.reshape(SLOTS, grp_count, owner_rows, chunk),
            "grp",
            split_axis=1,
            concat_axis=1,
            tiled=True,
        )
        pieces.append(
            jnp.einsum(
                "nsg,sgrc->rnc", onehot, arrived, precision=lax.Precision.HIGHEST, preferred_element_type=jnp.float32
            )
        )
    summed = jnp.concatenate(pieces, axis=2)
    return residual_in + summed


def solution(mesh):
    in_specs = (
        P(None, "blk", None),
        P(None, "blk"),
        P(("blk", "grp"), None, None),
        P(),
        P(),
        P(("blk", "grp"), None, None),
    )
    out_specs = P(("blk", "grp"), None, None)
    return jax.shard_map(shards, mesh=mesh, in_specs=in_specs, out_specs=out_specs, check_vma=False)
```

```python
import functools

import jax
import jax.numpy as jnp
from jax import lax
from jax.experimental import pallas as pl
from jax.experimental.pallas import tpu as pltpu
from jax.sharding import PartitionSpec as P

SLOTS = 4
CHUNKS = 4


def slot_of(column_ab):
    tiles = column_ab.shape[0]
    order = jnp.arange(tiles).reshape((tiles,) + (1,) * (column_ab.ndim - 1))
    same = column_ab[:, None] == column_ab[None, :]
    first = jnp.argmax(same, axis=1)
    is_first = first == order
    earlier = order[None, :] < first[:, None]
    return jnp.sum(earlier & is_first[None, :], axis=1).astype(jnp.int32)


def gather_kernel(count, source, gathered, send_sems, recv_sems, local_sem):
    me = lax.axis_index("blk")
    column = lax.axis_index("grp")
    ring = count // 2
    base = (me // ring) * ring
    half = source.shape[0] // 2
    pieces = (pl.ds(0, half), pl.ds(half, half))

    def along(step):
        return base + lax.rem(me - base + step + ring, ring)

    def across(device):
        return lax.rem(device + ring, count)

    partner, right, left, opposite = across(me), along(1), along(-1), along(2)
    local = pltpu.make_async_copy(source, gathered.at[me], local_sem)
    local.start()

    def transfer(origin, target, slot, piece=None):
        src = source if origin is me else gathered.at[origin]
        dst = gathered.at[origin]
        if piece is not None:
            src, dst = src.at[pieces[piece]], dst.at[pieces[piece]]
        return pltpu.make_async_remote_copy(
            src_ref=src,
            dst_ref=dst,
            send_sem=send_sems.at[slot],
            recv_sem=recv_sems.at[origin, 0 if piece is None else piece],
            device_id=(target, column),
            device_id_type=pl.DeviceIdType.MESH,
        )

    sent = [transfer(me, partner, 0), transfer(me, right, 1), transfer(me, left, 2)]
    for copy in sent:
        copy.start()
    relays = [
        (partner, partner, ((right, 3, None), (left, 4, None))),
        (left, left, ((right, 5, 0),)),
        (right, right, ((left, 6, 1),)),
        (across(left), left, ((right, 7, 0),)),
        (across(right), right, ((left, 8, 1),)),
    ]
    for origin, sender, onward in relays:
        transfer(origin, sender, 0).wait_recv()
        for target, slot, piece in onward:
            copy = transfer(origin, target, slot, piece)
            copy.start()
            sent.append(copy)
    for origin in (opposite, across(opposite)):
        transfer(origin, left, 0, 0).wait_recv()
        transfer(origin, right, 0, 1).wait_recv()
    for copy in sent:
        copy.wait_send()
    local.wait()


def gather_blk(piece):
    count = lax.axis_size("blk")
    rows, width = piece.shape
    return pl.pallas_call(
        functools.partial(gather_kernel, count),
        out_shape=jax.ShapeDtypeStruct((count, rows, width), piece.dtype),
        in_specs=[pl.BlockSpec(memory_space=pl.ANY)],
        out_specs=pl.BlockSpec(memory_space=pl.ANY),
        scratch_shapes=[
            pltpu.SemaphoreType.DMA((count + 1,)),
            pltpu.SemaphoreType.DMA((count, 2)),
            pltpu.SemaphoreType.DMA(()),
        ],
        compiler_params=pltpu.CompilerParams(has_side_effects=True),
        cost_estimate=pl.CostEstimate(flops=0, bytes_accessed=2 * count * rows * width * 2, transcendentals=0),
    )(piece)


def shards(amplitudes, pair_screen, integrals, tile_ab, tile_cd, residual_in):
    grp_count = lax.axis_size("grp")
    grp_position = lax.axis_index("grp")
    owner_rows, ab_tiles, tile_width = residual_in.shape
    group_rows = amplitudes.shape[1]
    row_mask = jnp.repeat(pair_screen, owner_rows, axis=1).astype(jnp.bfloat16)
    masked = amplitudes * row_mask[:, :, None]
    column_cd = lax.dynamic_index_in_dim(tile_cd, grp_position, 1, keepdims=False)
    column_ab = lax.dynamic_index_in_dim(tile_ab, grp_position, 1, keepdims=False)
    column_slot = slot_of(column_ab)
    all_slot = slot_of(tile_ab)
    slot_hit = all_slot[:, None, :] == jnp.arange(SLOTS)[None, :, None]
    ab_hit = tile_ab[None, :, :] == jnp.arange(ab_tiles)[:, None, None]
    onehot = jnp.any(ab_hit[:, :, None, :] & slot_hit[None, :, :, :], axis=1).astype(jnp.float32)
    chunk = tile_width // CHUNKS
    chunked = jnp.transpose(integrals.reshape(integrals.shape[1], CHUNKS, chunk), (1, 0, 2))
    pieces = []
    for part in range(CHUNKS):
        portion = gather_blk(chunked[part])
        running = jnp.zeros((SLOTS, group_rows, chunk), jnp.float32)
        for offset in range(portion.shape[0]):
            rows_in = lax.dynamic_index_in_dim(masked, column_cd[offset], 0, keepdims=False)
            product = jnp.dot(rows_in, portion[offset], preferred_element_type=jnp.float32)
            slot = column_slot[offset]
            earlier = lax.dynamic_index_in_dim(running, slot, 0, keepdims=False)
            running = lax.dynamic_update_index_in_dim(running, earlier + product, slot, 0)
        arrived = lax.all_to_all(
            running.reshape(SLOTS, grp_count, owner_rows, chunk),
            "grp",
            split_axis=1,
            concat_axis=1,
            tiled=True,
        )
        pieces.append(
            jnp.einsum(
                "nsg,sgrc->rnc", onehot, arrived, precision=lax.Precision.HIGHEST, preferred_element_type=jnp.float32
            )
        )
    summed = jnp.concatenate(pieces, axis=2)
    return residual_in + summed


def solution(mesh):
    in_specs = (
        P(None, "blk", None),
        P(None, "blk"),
        P(("blk", "grp"), None, None),
        P(),
        P(),
        P(("blk", "grp"), None, None),
    )
    out_specs = P(("blk", "grp"), None, None)
    return jax.shard_map(shards, mesh=mesh, in_specs=in_specs, out_specs=out_specs, check_vma=False)
```

```python
import functools

import jax
import jax.numpy as jnp
from jax import lax
from jax.experimental import pallas as pl
from jax.experimental.pallas import tpu as pltpu
from jax.sharding import PartitionSpec as P

SLOTS = 4
CHUNKS = 4


def slot_of(column_ab):
    tiles = column_ab.shape[0]
    order = jnp.arange(tiles).reshape((tiles,) + (1,) * (column_ab.ndim - 1))
    same = column_ab[:, None] == column_ab[None, :]
    first = jnp.argmax(same, axis=1)
    is_first = first == order
    earlier = order[None, :] < first[:, None]
    return jnp.sum(earlier & is_first[None, :], axis=1).astype(jnp.int32)


def gather_kernel(count, source, gathered, send_sems, recv_sems, local_sem):
    me = lax.axis_index("blk")
    column = lax.axis_index("grp")
    ring = count // 2
    base = (me // ring) * ring
    half = source.shape[0] // 2
    pieces = (pl.ds(0, half), pl.ds(half, half))

    def along(step):
        return base + lax.rem(me - base + step + ring, ring)

    def across(device):
        return lax.rem(device + ring, count)

    partner, right, left, opposite = across(me), along(1), along(-1), along(2)
    local = pltpu.make_async_copy(source, gathered.at[me], local_sem)
    local.start()

    def transfer(origin, target, slot, piece=None):
        src = source if origin is me else gathered.at[origin]
        dst = gathered.at[origin]
        if piece is not None:
            src, dst = src.at[pieces[piece]], dst.at[pieces[piece]]
        return pltpu.make_async_remote_copy(
            src_ref=src,
            dst_ref=dst,
            send_sem=send_sems.at[slot],
            recv_sem=recv_sems.at[origin, 0 if piece is None else piece],
            device_id=(target, column),
            device_id_type=pl.DeviceIdType.MESH,
        )

    sent = [transfer(me, partner, 0), transfer(me, right, 1), transfer(me, left, 2)]
    for copy in sent:
        copy.start()
    relays = [
        (partner, partner, ((right, 3, None), (left, 4, None))),
        (left, left, ((right, 5, 0),)),
        (right, right, ((left, 6, 1),)),
        (across(left), left, ((right, 7, 0),)),
        (across(right), right, ((left, 8, 1),)),
    ]
    for origin, sender, onward in relays:
        transfer(origin, sender, 0).wait_recv()
        for target, slot, piece in onward:
            copy = transfer(origin, target, slot, piece)
            copy.start()
            sent.append(copy)
    for origin in (opposite, across(opposite)):
        transfer(origin, left, 0, 0).wait_recv()
        transfer(origin, right, 0, 1).wait_recv()
    for copy in sent:
        copy.wait_send()
    local.wait()


def gather_blk(piece):
    count = lax.axis_size("blk")
    rows, width = piece.shape
    return pl.pallas_call(
        functools.partial(gather_kernel, count),
        out_shape=jax.ShapeDtypeStruct((count, rows, width), piece.dtype),
        in_specs=[pl.BlockSpec(memory_space=pl.ANY)],
        out_specs=pl.BlockSpec(memory_space=pl.ANY),
        scratch_shapes=[
            pltpu.SemaphoreType.DMA((count + 1,)),
            pltpu.SemaphoreType.DMA((count, 2)),
            pltpu.SemaphoreType.DMA(()),
        ],
        compiler_params=pltpu.CompilerParams(has_side_effects=True),
        cost_estimate=pl.CostEstimate(flops=0, bytes_accessed=2 * count * rows * width * 2, transcendentals=0),
    )(piece)


def shards(amplitudes, pair_screen, integrals, tile_ab, tile_cd, residual_in):
    grp_count = lax.axis_size("grp")
    grp_position = lax.axis_index("grp")
    owner_rows, ab_tiles, tile_width = residual_in.shape
    group_rows = amplitudes.shape[1]
    row_mask = jnp.repeat(pair_screen, owner_rows, axis=1).astype(jnp.bfloat16)
    masked = amplitudes * row_mask[:, :, None]
    column_cd = lax.dynamic_index_in_dim(tile_cd, grp_position, 1, keepdims=False)
    column_ab = lax.dynamic_index_in_dim(tile_ab, grp_position, 1, keepdims=False)
    column_slot = slot_of(column_ab)
    all_slot = slot_of(tile_ab)
    slot_hit = all_slot[:, None, :] == jnp.arange(SLOTS)[None, :, None]
    ab_hit = tile_ab[None, :, :] == jnp.arange(ab_tiles)[:, None, None]
    onehot = jnp.any(ab_hit[:, :, None, :] & slot_hit[None, :, :, :], axis=1).astype(jnp.float32)
    chunk = tile_width // CHUNKS
    chunked = jnp.transpose(integrals.reshape(integrals.shape[1], CHUNKS, chunk), (1, 0, 2))
    halves = jnp.transpose(integrals.reshape(integrals.shape[1], 2, tile_width // 2), (1, 0, 2))
    offloaded = lax.all_gather(halves[0:1], "blk", axis=0, tiled=True)
    parts = [gather_blk(chunked[part]) for part in range(CHUNKS // 2, CHUNKS)] + [offloaded]
    pieces = []
    for portion in parts:
        width = portion.shape[2]
        running = jnp.zeros((SLOTS, group_rows, width), jnp.float32)
        for offset in range(portion.shape[0]):
            rows_in = lax.dynamic_index_in_dim(masked, column_cd[offset], 0, keepdims=False)
            product = jnp.dot(rows_in, portion[offset], preferred_element_type=jnp.float32)
            slot = column_slot[offset]
            earlier = lax.dynamic_index_in_dim(running, slot, 0, keepdims=False)
            running = lax.dynamic_update_index_in_dim(running, earlier + product, slot, 0)
        arrived = lax.all_to_all(
            running.reshape(SLOTS, grp_count, owner_rows, width),
            "grp",
            split_axis=1,
            concat_axis=1,
            tiled=True,
        )
        pieces.append(
            jnp.einsum(
                "nsg,sgrc->rnc", onehot, arrived, precision=lax.Precision.HIGHEST, preferred_element_type=jnp.float32
            )
        )
    pieces = pieces[-1:] + pieces[:-1]
    summed = jnp.concatenate(pieces, axis=2)
    return residual_in + summed


def solution(mesh):
    in_specs = (
        P(None, "blk", None),
        P(None, "blk"),
        P(("blk", "grp"), None, None),
        P(),
        P(),
        P(("blk", "grp"), None, None),
    )
    out_specs = P(("blk", "grp"), None, None)
    return jax.shard_map(shards, mesh=mesh, in_specs=in_specs, out_specs=out_specs, check_vma=False)
```

```python
import functools

import jax
import jax.numpy as jnp
from jax import lax
from jax.experimental import pallas as pl
from jax.experimental.pallas import tpu as pltpu
from jax.sharding import PartitionSpec as P

SLOTS = 4
CHUNKS = 4


def slot_of(column_ab):
    tiles = column_ab.shape[0]
    order = jnp.arange(tiles).reshape((tiles,) + (1,) * (column_ab.ndim - 1))
    same = column_ab[:, None] == column_ab[None, :]
    first = jnp.argmax(same, axis=1)
    is_first = first == order
    earlier = order[None, :] < first[:, None]
    return jnp.sum(earlier & is_first[None, :], axis=1).astype(jnp.int32)


def gather_kernel(count, source, gathered, send_sems, recv_sems, local_sem):
    me = lax.axis_index("blk")
    column = lax.axis_index("grp")
    ring = count // 2
    base = (me // ring) * ring
    half = source.shape[0] // 2
    pieces = (pl.ds(0, half), pl.ds(half, half))

    def along(step):
        return base + lax.rem(me - base + step + ring, ring)

    def across(device):
        return lax.rem(device + ring, count)

    partner, right, left, opposite = across(me), along(1), along(-1), along(2)
    local = pltpu.make_async_copy(source, gathered.at[me], local_sem)
    local.start()

    def transfer(origin, target, slot, piece=None):
        src = source if origin is me else gathered.at[origin]
        dst = gathered.at[origin]
        if piece is not None:
            src, dst = src.at[pieces[piece]], dst.at[pieces[piece]]
        return pltpu.make_async_remote_copy(
            src_ref=src,
            dst_ref=dst,
            send_sem=send_sems.at[slot],
            recv_sem=recv_sems.at[origin, 0 if piece is None else piece],
            device_id=(target, column),
            device_id_type=pl.DeviceIdType.MESH,
        )

    sent = [transfer(me, partner, 0), transfer(me, right, 1), transfer(me, left, 2)]
    for copy in sent:
        copy.start()
    relays = [
        (partner, partner, ((right, 3, None), (left, 4, None))),
        (left, left, ((right, 5, 0),)),
        (right, right, ((left, 6, 1),)),
        (across(left), left, ((right, 7, 0),)),
        (across(right), right, ((left, 8, 1),)),
    ]
    for origin, sender, onward in relays:
        transfer(origin, sender, 0).wait_recv()
        for target, slot, piece in onward:
            copy = transfer(origin, target, slot, piece)
            copy.start()
            sent.append(copy)
    for origin in (opposite, across(opposite)):
        transfer(origin, left, 0, 0).wait_recv()
        transfer(origin, right, 0, 1).wait_recv()
    for copy in sent:
        copy.wait_send()
    local.wait()


def gather_blk(piece):
    count = lax.axis_size("blk")
    rows, width = piece.shape
    return pl.pallas_call(
        functools.partial(gather_kernel, count),
        out_shape=jax.ShapeDtypeStruct((count, rows, width), piece.dtype),
        in_specs=[pl.BlockSpec(memory_space=pl.ANY)],
        out_specs=pl.BlockSpec(memory_space=pl.ANY),
        scratch_shapes=[
            pltpu.SemaphoreType.DMA((count + 1,)),
            pltpu.SemaphoreType.DMA((count, 2)),
            pltpu.SemaphoreType.DMA(()),
        ],
        compiler_params=pltpu.CompilerParams(has_side_effects=True),
        cost_estimate=pl.CostEstimate(flops=0, bytes_accessed=2 * count * rows * width * 2, transcendentals=0),
    )(piece)


def shards(amplitudes, pair_screen, integrals, tile_ab, tile_cd, residual_in):
    grp_count = lax.axis_size("grp")
    grp_position = lax.axis_index("grp")
    owner_rows, ab_tiles, tile_width = residual_in.shape
    group_rows = amplitudes.shape[1]
    row_mask = jnp.repeat(pair_screen, owner_rows, axis=1).astype(jnp.bfloat16)
    masked = amplitudes * row_mask[:, :, None]
    column_cd = lax.dynamic_index_in_dim(tile_cd, grp_position, 1, keepdims=False)
    column_ab = lax.dynamic_index_in_dim(tile_ab, grp_position, 1, keepdims=False)
    column_slot = slot_of(column_ab)
    all_slot = slot_of(tile_ab)
    slot_hit = all_slot[:, None, :] == jnp.arange(SLOTS)[None, :, None]
    ab_hit = tile_ab[None, :, :] == jnp.arange(ab_tiles)[:, None, None]
    onehot = jnp.any(ab_hit[:, :, None, :] & slot_hit[None, :, :, :], axis=1).astype(jnp.float32)
    chunk = tile_width // CHUNKS
    chunked = jnp.transpose(integrals.reshape(integrals.shape[1], CHUNKS, chunk), (1, 0, 2))
    halves = jnp.transpose(integrals.reshape(integrals.shape[1], 2, tile_width // 2), (1, 0, 2))
    offloaded = lax.all_gather(halves[0:1], "blk", axis=0, tiled=True)
    pieces = []

    def contract(portion):
        width = portion.shape[2]
        running = jnp.zeros((SLOTS, group_rows, width), jnp.float32)
        for offset in range(portion.shape[0]):
            rows_in = lax.dynamic_index_in_dim(masked, column_cd[offset], 0, keepdims=False)
            product = jnp.dot(rows_in, portion[offset], preferred_element_type=jnp.float32)
            slot = column_slot[offset]
            earlier = lax.dynamic_index_in_dim(running, slot, 0, keepdims=False)
            running = lax.dynamic_update_index_in_dim(running, earlier + product, slot, 0)
        return running

    def exchange(running):
        width = running.shape[2]
        arrived = lax.all_to_all(
            running.reshape(SLOTS, grp_count, owner_rows, width),
            "grp",
            split_axis=1,
            concat_axis=1,
            tiled=True,
        )
        return jnp.einsum(
            "nsg,sgrc->rnc", onehot, arrived, precision=lax.Precision.HIGHEST, preferred_element_type=jnp.float32
        )

    first = exchange(contract(gather_blk(chunked[CHUNKS // 2])))
    offloaded_sums = contract(offloaded)
    offloaded_sums, last_input = lax.optimization_barrier((offloaded_sums, chunked[CHUNKS - 1]))
    pieces = [exchange(offloaded_sums), first, exchange(contract(gather_blk(last_input)))]
    summed = jnp.concatenate(pieces, axis=2)
    return residual_in + summed


def solution(mesh):
    in_specs = (
        P(None, "blk", None),
        P(None, "blk"),
        P(("blk", "grp"), None, None),
        P(),
        P(),
        P(("blk", "grp"), None, None),
    )
    out_specs = P(("blk", "grp"), None, None)
    return jax.shard_map(shards, mesh=mesh, in_specs=in_specs, out_specs=out_specs, check_vma=False)
```

```python
import functools

import jax
import jax.numpy as jnp
from jax import lax
from jax.experimental import pallas as pl
from jax.experimental.pallas import tpu as pltpu
from jax.sharding import PartitionSpec as P

SLOTS = 4
CHUNKS = 4


def slot_of(column_ab):
    tiles = column_ab.shape[0]
    order = jnp.arange(tiles).reshape((tiles,) + (1,) * (column_ab.ndim - 1))
    same = column_ab[:, None] == column_ab[None, :]
    first = jnp.argmax(same, axis=1)
    is_first = first == order
    earlier = order[None, :] < first[:, None]
    return jnp.sum(earlier & is_first[None, :], axis=1).astype(jnp.int32)


def gather_kernel(count, source, gathered, send_sems, recv_sems, local_sem):
    me = lax.axis_index("blk")
    column = lax.axis_index("grp")
    ring = count // 2
    base = (me // ring) * ring
    half = source.shape[0] // 2
    pieces = (pl.ds(0, half), pl.ds(half, half))

    def along(step):
        return base + lax.rem(me - base + step + ring, ring)

    def across(device):
        return lax.rem(device + ring, count)

    partner, right, left, opposite = across(me), along(1), along(-1), along(2)
    local = pltpu.make_async_copy(source, gathered.at[me], local_sem)
    local.start()

    def transfer(origin, target, slot, piece=None):
        src = source if origin is me else gathered.at[origin]
        dst = gathered.at[origin]
        if piece is not None:
            src, dst = src.at[pieces[piece]], dst.at[pieces[piece]]
        return pltpu.make_async_remote_copy(
            src_ref=src,
            dst_ref=dst,
            send_sem=send_sems.at[slot],
            recv_sem=recv_sems.at[origin, 0 if piece is None else piece],
            device_id=(target, column),
            device_id_type=pl.DeviceIdType.MESH,
        )

    sent = [transfer(me, partner, 0), transfer(me, right, 1), transfer(me, left, 2)]
    for copy in sent:
        copy.start()
    relays = [
        (partner, partner, ((right, 3, None), (left, 4, None))),
        (left, left, ((right, 5, 0),)),
        (right, right, ((left, 6, 1),)),
        (across(left), left, ((right, 7, 0),)),
        (across(right), right, ((left, 8, 1),)),
    ]
    for origin, sender, onward in relays:
        transfer(origin, sender, 0).wait_recv()
        for target, slot, piece in onward:
            copy = transfer(origin, target, slot, piece)
            copy.start()
            sent.append(copy)
    for origin in (opposite, across(opposite)):
        transfer(origin, left, 0, 0).wait_recv()
        transfer(origin, right, 0, 1).wait_recv()
    for copy in sent:
        copy.wait_send()
    local.wait()


def gather_blk(piece):
    count = lax.axis_size("blk")
    rows, width = piece.shape
    return pl.pallas_call(
        functools.partial(gather_kernel, count),
        out_shape=jax.ShapeDtypeStruct((count, rows, width), piece.dtype),
        in_specs=[pl.BlockSpec(memory_space=pl.ANY)],
        out_specs=pl.BlockSpec(memory_space=pl.ANY),
        scratch_shapes=[
            pltpu.SemaphoreType.DMA((count + 1,)),
            pltpu.SemaphoreType.DMA((count, 2)),
            pltpu.SemaphoreType.DMA(()),
        ],
        compiler_params=pltpu.CompilerParams(has_side_effects=True),
        cost_estimate=pl.CostEstimate(flops=0, bytes_accessed=2 * count * rows * width * 2, transcendentals=0),
    )(piece)


def shards(amplitudes, pair_screen, integrals, tile_ab, tile_cd, residual_in):
    grp_count = lax.axis_size("grp")
    grp_position = lax.axis_index("grp")
    owner_rows, ab_tiles, tile_width = residual_in.shape
    group_rows = amplitudes.shape[1]
    row_mask = jnp.repeat(pair_screen, owner_rows, axis=1).astype(jnp.bfloat16)
    masked = amplitudes * row_mask[:, :, None]
    column_cd = lax.dynamic_index_in_dim(tile_cd, grp_position, 1, keepdims=False)
    column_ab = lax.dynamic_index_in_dim(tile_ab, grp_position, 1, keepdims=False)
    column_slot = slot_of(column_ab)
    all_slot = slot_of(tile_ab)
    slot_hit = all_slot[:, None, :] == jnp.arange(SLOTS)[None, :, None]
    ab_hit = tile_ab[None, :, :] == jnp.arange(ab_tiles)[:, None, None]
    onehot = jnp.any(ab_hit[:, :, None, :] & slot_hit[None, :, :, :], axis=1).astype(jnp.float32)
    chunk = tile_width // CHUNKS
    chunked = jnp.transpose(integrals.reshape(integrals.shape[1], CHUNKS, chunk), (1, 0, 2))
    offloaded = lax.all_gather(chunked[0:1], "blk", axis=0, tiled=True)
    parts = [gather_blk(chunked[part]) for part in range(1, CHUNKS)] + [offloaded]
    pieces = []
    for portion in parts:
        width = portion.shape[2]
        running = jnp.zeros((SLOTS, group_rows, width), jnp.float32)
        for offset in range(portion.shape[0]):
            rows_in = lax.dynamic_index_in_dim(masked, column_cd[offset], 0, keepdims=False)
            product = jnp.dot(rows_in, portion[offset], preferred_element_type=jnp.float32)
            slot = column_slot[offset]
            earlier = lax.dynamic_index_in_dim(running, slot, 0, keepdims=False)
            running = lax.dynamic_update_index_in_dim(running, earlier + product, slot, 0)
        arrived = lax.all_to_all(
            running.reshape(SLOTS, grp_count, owner_rows, width),
            "grp",
            split_axis=1,
            concat_axis=1,
            tiled=True,
        )
        pieces.append(
            jnp.einsum(
                "nsg,sgrc->rnc", onehot, arrived, precision=lax.Precision.HIGHEST, preferred_element_type=jnp.float32
            )
        )
    pieces = pieces[-1:] + pieces[:-1]
    summed = jnp.concatenate(pieces, axis=2)
    return residual_in + summed


def solution(mesh):
    in_specs = (
        P(None, "blk", None),
        P(None, "blk"),
        P(("blk", "grp"), None, None),
        P(),
        P(),
        P(("blk", "grp"), None, None),
    )
    out_specs = P(("blk", "grp"), None, None)
    return jax.shard_map(shards, mesh=mesh, in_specs=in_specs, out_specs=out_specs, check_vma=False)
```

```python
import functools

import jax
import jax.numpy as jnp
from jax import lax
from jax.experimental import pallas as pl
from jax.experimental.pallas import tpu as pltpu
from jax.sharding import PartitionSpec as P

SLOTS = 4
CHUNKS = 4


def slot_of(column_ab):
    tiles = column_ab.shape[0]
    order = jnp.arange(tiles).reshape((tiles,) + (1,) * (column_ab.ndim - 1))
    same = column_ab[:, None] == column_ab[None, :]
    first = jnp.argmax(same, axis=1)
    is_first = first == order
    earlier = order[None, :] < first[:, None]
    return jnp.sum(earlier & is_first[None, :], axis=1).astype(jnp.int32)


def gather_kernel(count, source, gathered, send_sems, recv_sems, local_sem):
    me = lax.axis_index("blk")
    column = lax.axis_index("grp")
    ring = count // 2
    base = (me // ring) * ring
    half = source.shape[0] // 2
    pieces = (pl.ds(0, half), pl.ds(half, half))

    def along(step):
        return base + lax.rem(me - base + step + ring, ring)

    def across(device):
        return lax.rem(device + ring, count)

    partner, right, left, opposite = across(me), along(1), along(-1), along(2)
    local = pltpu.make_async_copy(source, gathered.at[me], local_sem)
    local.start()

    def transfer(origin, target, slot, piece=None):
        src = source if origin is me else gathered.at[origin]
        dst = gathered.at[origin]
        if piece is not None:
            src, dst = src.at[pieces[piece]], dst.at[pieces[piece]]
        return pltpu.make_async_remote_copy(
            src_ref=src,
            dst_ref=dst,
            send_sem=send_sems.at[slot],
            recv_sem=recv_sems.at[origin, 0 if piece is None else piece],
            device_id=(target, column),
            device_id_type=pl.DeviceIdType.MESH,
        )

    sent = [transfer(me, partner, 0), transfer(me, right, 1), transfer(me, left, 2)]
    for copy in sent:
        copy.start()
    relays = [
        (partner, partner, ((right, 3, None), (left, 4, None))),
        (left, left, ((right, 5, 0),)),
        (right, right, ((left, 6, 1),)),
        (across(left), left, ((right, 7, 0),)),
        (across(right), right, ((left, 8, 1),)),
    ]
    for origin, sender, onward in relays:
        transfer(origin, sender, 0).wait_recv()
        for target, slot, piece in onward:
            copy = transfer(origin, target, slot, piece)
            copy.start()
            sent.append(copy)
    for origin in (opposite, across(opposite)):
        transfer(origin, left, 0, 0).wait_recv()
        transfer(origin, right, 0, 1).wait_recv()
    for copy in sent:
        copy.wait_send()
    local.wait()


def gather_blk(piece):
    count = lax.axis_size("blk")
    rows, width = piece.shape
    return pl.pallas_call(
        functools.partial(gather_kernel, count),
        out_shape=jax.ShapeDtypeStruct((count, rows, width), piece.dtype),
        in_specs=[pl.BlockSpec(memory_space=pl.ANY)],
        out_specs=pl.BlockSpec(memory_space=pl.ANY),
        scratch_shapes=[
            pltpu.SemaphoreType.DMA((count + 1,)),
            pltpu.SemaphoreType.DMA((count, 2)),
            pltpu.SemaphoreType.DMA(()),
        ],
        compiler_params=pltpu.CompilerParams(has_side_effects=True),
        cost_estimate=pl.CostEstimate(flops=0, bytes_accessed=2 * count * rows * width * 2, transcendentals=0),
    )(piece)


def shards(amplitudes, pair_screen, integrals, tile_ab, tile_cd, residual_in):
    grp_count = lax.axis_size("grp")
    grp_position = lax.axis_index("grp")
    owner_rows, ab_tiles, tile_width = residual_in.shape
    group_rows = amplitudes.shape[1]
    row_mask = jnp.repeat(pair_screen, owner_rows, axis=1).astype(jnp.bfloat16)
    masked = amplitudes * row_mask[:, :, None]
    column_cd = lax.dynamic_index_in_dim(tile_cd, grp_position, 1, keepdims=False)
    column_ab = lax.dynamic_index_in_dim(tile_ab, grp_position, 1, keepdims=False)
    column_slot = slot_of(column_ab)
    all_slot = slot_of(tile_ab)
    slot_hit = all_slot[:, None, :] == jnp.arange(SLOTS)[None, :, None]
    ab_hit = tile_ab[None, :, :] == jnp.arange(ab_tiles)[:, None, None]
    onehot = jnp.any(ab_hit[:, :, None, :] & slot_hit[None, :, :, :], axis=1).astype(jnp.float32)
    chunk = tile_width // CHUNKS
    chunked = jnp.transpose(integrals.reshape(integrals.shape[1], CHUNKS, chunk), (1, 0, 2))
    halves = jnp.transpose(integrals.reshape(integrals.shape[1], 2, tile_width // 2), (1, 0, 2))
    offloaded = lax.all_gather(halves[0:1], "blk", axis=0, tiled=True)
    parts = [gather_blk(halves[1]), offloaded]
    pieces = []
    for portion in parts:
        width = portion.shape[2]
        running = jnp.zeros((SLOTS, group_rows, width), jnp.float32)
        for offset in range(portion.shape[0]):
            rows_in = lax.dynamic_index_in_dim(masked, column_cd[offset], 0, keepdims=False)
            product = jnp.dot(rows_in, portion[offset], preferred_element_type=jnp.float32)
            slot = column_slot[offset]
            earlier = lax.dynamic_index_in_dim(running, slot, 0, keepdims=False)
            running = lax.dynamic_update_index_in_dim(running, earlier + product, slot, 0)
        arrived = lax.all_to_all(
            running.reshape(SLOTS, grp_count, owner_rows, width),
            "grp",
            split_axis=1,
            concat_axis=1,
            tiled=True,
        )
        pieces.append(
            jnp.einsum(
                "nsg,sgrc->rnc", onehot, arrived, precision=lax.Precision.HIGHEST, preferred_element_type=jnp.float32
            )
        )
    pieces = pieces[-1:] + pieces[:-1]
    summed = jnp.concatenate(pieces, axis=2)
    return residual_in + summed


def solution(mesh):
    in_specs = (
        P(None, "blk", None),
        P(None, "blk"),
        P(("blk", "grp"), None, None),
        P(),
        P(),
        P(("blk", "grp"), None, None),
    )
    out_specs = P(("blk", "grp"), None, None)
    return jax.shard_map(shards, mesh=mesh, in_specs=in_specs, out_specs=out_specs, check_vma=False)
```

```python
import functools

import jax
import jax.numpy as jnp
from jax import lax
from jax.experimental import pallas as pl
from jax.experimental.pallas import tpu as pltpu
from jax.sharding import PartitionSpec as P

SLOTS = 4
CHUNKS = 4


def slot_of(column_ab):
    tiles = column_ab.shape[0]
    order = jnp.arange(tiles).reshape((tiles,) + (1,) * (column_ab.ndim - 1))
    same = column_ab[:, None] == column_ab[None, :]
    first = jnp.argmax(same, axis=1)
    is_first = first == order
    earlier = order[None, :] < first[:, None]
    return jnp.sum(earlier & is_first[None, :], axis=1).astype(jnp.int32)


def gather_kernel(count, source, gathered, send_sems, recv_sems, local_sem):
    me = lax.axis_index("blk")
    column = lax.axis_index("grp")
    ring = count // 2
    base = (me // ring) * ring
    half = source.shape[0] // 2
    pieces = (pl.ds(0, half), pl.ds(half, half))

    def along(step):
        return base + lax.rem(me - base + step + ring, ring)

    def across(device):
        return lax.rem(device + ring, count)

    partner, right, left, opposite = across(me), along(1), along(-1), along(2)
    local = pltpu.make_async_copy(source, gathered.at[me], local_sem)
    local.start()

    def transfer(origin, target, slot, piece=None):
        src = source if origin is me else gathered.at[origin]
        dst = gathered.at[origin]
        if piece is not None:
            src, dst = src.at[pieces[piece]], dst.at[pieces[piece]]
        return pltpu.make_async_remote_copy(
            src_ref=src,
            dst_ref=dst,
            send_sem=send_sems.at[slot],
            recv_sem=recv_sems.at[origin, 0 if piece is None else piece],
            device_id=(target, column),
            device_id_type=pl.DeviceIdType.MESH,
        )

    sent = [transfer(me, partner, 0), transfer(me, right, 1), transfer(me, left, 2)]
    for copy in sent:
        copy.start()
    relays = [
        (partner, partner, ((right, 3, None), (left, 4, None))),
        (left, left, ((right, 5, 0),)),
        (right, right, ((left, 6, 1),)),
        (across(left), left, ((right, 7, 0),)),
        (across(right), right, ((left, 8, 1),)),
    ]
    for origin, sender, onward in relays:
        transfer(origin, sender, 0).wait_recv()
        for target, slot, piece in onward:
            copy = transfer(origin, target, slot, piece)
            copy.start()
            sent.append(copy)
    for origin in (opposite, across(opposite)):
        transfer(origin, left, 0, 0).wait_recv()
        transfer(origin, right, 0, 1).wait_recv()
    for copy in sent:
        copy.wait_send()
    local.wait()


def gather_blk(piece):
    count = lax.axis_size("blk")
    rows, width = piece.shape
    return pl.pallas_call(
        functools.partial(gather_kernel, count),
        out_shape=jax.ShapeDtypeStruct((count, rows, width), piece.dtype),
        in_specs=[pl.BlockSpec(memory_space=pl.ANY)],
        out_specs=pl.BlockSpec(memory_space=pl.ANY),
        scratch_shapes=[
            pltpu.SemaphoreType.DMA((count + 1,)),
            pltpu.SemaphoreType.DMA((count, 2)),
            pltpu.SemaphoreType.DMA(()),
        ],
        compiler_params=pltpu.CompilerParams(has_side_effects=True),
        cost_estimate=pl.CostEstimate(flops=0, bytes_accessed=2 * count * rows * width * 2, transcendentals=0),
    )(piece)


def shards(amplitudes, pair_screen, integrals, tile_ab, tile_cd, residual_in):
    grp_count = lax.axis_size("grp")
    grp_position = lax.axis_index("grp")
    owner_rows, ab_tiles, tile_width = residual_in.shape
    group_rows = amplitudes.shape[1]
    row_mask = jnp.repeat(pair_screen, owner_rows, axis=1).astype(jnp.bfloat16)
    masked = amplitudes * row_mask[:, :, None]
    column_cd = lax.dynamic_index_in_dim(tile_cd, grp_position, 1, keepdims=False)
    column_ab = lax.dynamic_index_in_dim(tile_ab, grp_position, 1, keepdims=False)
    column_slot = slot_of(column_ab)
    all_slot = slot_of(tile_ab)
    slot_hit = all_slot[:, None, :] == jnp.arange(SLOTS)[None, :, None]
    ab_hit = tile_ab[None, :, :] == jnp.arange(ab_tiles)[:, None, None]
    onehot = jnp.any(ab_hit[:, :, None, :] & slot_hit[None, :, :, :], axis=1).astype(jnp.float32)
    chunk = tile_width // CHUNKS
    chunked = jnp.transpose(integrals.reshape(integrals.shape[1], CHUNKS, chunk), (1, 0, 2))
    split = 3 * tile_width // 8
    step = (tile_width - split) // 2
    offloaded = lax.all_gather(integrals[:, :, :split], "blk", axis=0, tiled=True)
    parts = [gather_blk(integrals[0, :, split + part * step : split + (part + 1) * step]) for part in range(2)]
    parts = parts + [offloaded]
    pieces = []
    for portion in parts:
        width = portion.shape[2]
        running = jnp.zeros((SLOTS, group_rows, width), jnp.float32)
        for offset in range(portion.shape[0]):
            rows_in = lax.dynamic_index_in_dim(masked, column_cd[offset], 0, keepdims=False)
            product = jnp.dot(rows_in, portion[offset], preferred_element_type=jnp.float32)
            slot = column_slot[offset]
            earlier = lax.dynamic_index_in_dim(running, slot, 0, keepdims=False)
            running = lax.dynamic_update_index_in_dim(running, earlier + product, slot, 0)
        arrived = lax.all_to_all(
            running.reshape(SLOTS, grp_count, owner_rows, width),
            "grp",
            split_axis=1,
            concat_axis=1,
            tiled=True,
        )
        pieces.append(
            jnp.einsum(
                "nsg,sgrc->rnc", onehot, arrived, precision=lax.Precision.HIGHEST, preferred_element_type=jnp.float32
            )
        )
    pieces = pieces[-1:] + pieces[:-1]
    summed = jnp.concatenate(pieces, axis=2)
    return residual_in + summed


def solution(mesh):
    in_specs = (
        P(None, "blk", None),
        P(None, "blk"),
        P(("blk", "grp"), None, None),
        P(),
        P(),
        P(("blk", "grp"), None, None),
    )
    out_specs = P(("blk", "grp"), None, None)
    return jax.shard_map(shards, mesh=mesh, in_specs=in_specs, out_specs=out_specs, check_vma=False)
```

```python
import functools

import jax
import jax.numpy as jnp
from jax import lax
from jax.experimental import pallas as pl
from jax.experimental.pallas import tpu as pltpu
from jax.sharding import PartitionSpec as P

SLOTS = 4
CHUNKS = 4


def slot_of(column_ab):
    tiles = column_ab.shape[0]
    order = jnp.arange(tiles).reshape((tiles,) + (1,) * (column_ab.ndim - 1))
    same = column_ab[:, None] == column_ab[None, :]
    first = jnp.argmax(same, axis=1)
    is_first = first == order
    earlier = order[None, :] < first[:, None]
    return jnp.sum(earlier & is_first[None, :], axis=1).astype(jnp.int32)


def gather_kernel(count, source, gathered, send_sems, recv_sems, local_sem):
    me = lax.axis_index("blk")
    column = lax.axis_index("grp")
    ring = count // 2
    base = (me // ring) * ring
    half = source.shape[0] // 2
    pieces = (pl.ds(0, half), pl.ds(half, half))

    def along(step):
        return base + lax.rem(me - base + step + ring, ring)

    def across(device):
        return lax.rem(device + ring, count)

    partner, right, left, opposite = across(me), along(1), along(-1), along(2)
    local = pltpu.make_async_copy(source, gathered.at[me], local_sem)
    local.start()

    def transfer(origin, target, slot, piece=None):
        src = source if origin is me else gathered.at[origin]
        dst = gathered.at[origin]
        if piece is not None:
            src, dst = src.at[pieces[piece]], dst.at[pieces[piece]]
        return pltpu.make_async_remote_copy(
            src_ref=src,
            dst_ref=dst,
            send_sem=send_sems.at[slot],
            recv_sem=recv_sems.at[origin, 0 if piece is None else piece],
            device_id=(target, column),
            device_id_type=pl.DeviceIdType.MESH,
        )

    sent = [transfer(me, partner, 0), transfer(me, right, 1), transfer(me, left, 2)]
    for copy in sent:
        copy.start()
    relays = [
        (partner, partner, ((right, 3, None), (left, 4, None))),
        (left, left, ((right, 5, 0),)),
        (right, right, ((left, 6, 1),)),
        (across(left), left, ((right, 7, 0),)),
        (across(right), right, ((left, 8, 1),)),
    ]
    for origin, sender, onward in relays:
        transfer(origin, sender, 0).wait_recv()
        for target, slot, piece in onward:
            copy = transfer(origin, target, slot, piece)
            copy.start()
            sent.append(copy)
    for origin in (opposite, across(opposite)):
        transfer(origin, left, 0, 0).wait_recv()
        transfer(origin, right, 0, 1).wait_recv()
    for copy in sent:
        copy.wait_send()
    local.wait()


def gather_blk(piece):
    count = lax.axis_size("blk")
    rows, width = piece.shape
    return pl.pallas_call(
        functools.partial(gather_kernel, count),
        out_shape=jax.ShapeDtypeStruct((count, rows, width), piece.dtype),
        in_specs=[pl.BlockSpec(memory_space=pl.ANY)],
        out_specs=pl.BlockSpec(memory_space=pl.ANY),
        scratch_shapes=[
            pltpu.SemaphoreType.DMA((count + 1,)),
            pltpu.SemaphoreType.DMA((count, 2)),
            pltpu.SemaphoreType.DMA(()),
        ],
        compiler_params=pltpu.CompilerParams(has_side_effects=True),
        cost_estimate=pl.CostEstimate(flops=0, bytes_accessed=2 * count * rows * width * 2, transcendentals=0),
    )(piece)


def shards(amplitudes, pair_screen, integrals, tile_ab, tile_cd, residual_in):
    grp_count = lax.axis_size("grp")
    grp_position = lax.axis_index("grp")
    owner_rows, ab_tiles, tile_width = residual_in.shape
    group_rows = amplitudes.shape[1]
    row_mask = jnp.repeat(pair_screen, owner_rows, axis=1).astype(jnp.bfloat16)
    masked = amplitudes * row_mask[:, :, None]
    column_cd = lax.dynamic_index_in_dim(tile_cd, grp_position, 1, keepdims=False)
    column_ab = lax.dynamic_index_in_dim(tile_ab, grp_position, 1, keepdims=False)
    column_slot = slot_of(column_ab)
    all_slot = slot_of(tile_ab)
    slot_hit = all_slot[:, None, :] == jnp.arange(SLOTS)[None, :, None]
    ab_hit = tile_ab[None, :, :] == jnp.arange(ab_tiles)[:, None, None]
    onehot = jnp.any(ab_hit[:, :, None, :] & slot_hit[None, :, :, :], axis=1).astype(jnp.float32)
    chunk = tile_width // CHUNKS
    chunked = jnp.transpose(integrals.reshape(integrals.shape[1], CHUNKS, chunk), (1, 0, 2))
    halves = jnp.transpose(integrals.reshape(integrals.shape[1], 2, tile_width // 2), (1, 0, 2))
    offloaded = lax.all_gather(halves[0:1], "blk", axis=0, tiled=True)
    def contract(portion):
        width = portion.shape[2]
        running = jnp.zeros((SLOTS, group_rows, width), jnp.float32)
        for offset in range(portion.shape[0]):
            rows_in = lax.dynamic_index_in_dim(masked, column_cd[offset], 0, keepdims=False)
            product = jnp.dot(rows_in, portion[offset], preferred_element_type=jnp.float32)
            slot = column_slot[offset]
            earlier = lax.dynamic_index_in_dim(running, slot, 0, keepdims=False)
            running = lax.dynamic_update_index_in_dim(running, earlier + product, slot, 0)
        return running

    def exchange(running):
        width = running.shape[2]
        return lax.all_to_all(
            running.reshape(SLOTS, grp_count, owner_rows, width),
            "grp",
            split_axis=1,
            concat_axis=1,
            tiled=True,
        )

    def accumulate(arrived):
        return jnp.einsum(
            "nsg,sgrc->rnc", onehot, arrived, precision=lax.Precision.HIGHEST, preferred_element_type=jnp.float32
        )

    early = exchange(contract(gather_blk(chunked[CHUNKS // 2])))
    late_sums = contract(gather_blk(chunked[CHUNKS - 1]))
    offloaded_arrived = exchange(contract(offloaded))
    late_sums, offloaded_arrived = lax.optimization_barrier((late_sums, offloaded_arrived))
    pieces = [accumulate(offloaded_arrived), accumulate(early), accumulate(exchange(late_sums))]
    summed = jnp.concatenate(pieces, axis=2)
    return residual_in + summed


def solution(mesh):
    in_specs = (
        P(None, "blk", None),
        P(None, "blk"),
        P(("blk", "grp"), None, None),
        P(),
        P(),
        P(("blk", "grp"), None, None),
    )
    out_specs = P(("blk", "grp"), None, None)
    return jax.shard_map(shards, mesh=mesh, in_specs=in_specs, out_specs=out_specs, check_vma=False)
```

```python
import functools

import jax
import jax.numpy as jnp
from jax import lax
from jax.experimental import pallas as pl
from jax.experimental.pallas import tpu as pltpu
from jax.sharding import PartitionSpec as P

SLOTS = 4
CHUNKS = 4


def slot_of(column_ab):
    tiles = column_ab.shape[0]
    order = jnp.arange(tiles).reshape((tiles,) + (1,) * (column_ab.ndim - 1))
    same = column_ab[:, None] == column_ab[None, :]
    first = jnp.argmax(same, axis=1)
    is_first = first == order
    earlier = order[None, :] < first[:, None]
    return jnp.sum(earlier & is_first[None, :], axis=1).astype(jnp.int32)


def gather_kernel(count, source, gathered, send_sems, recv_sems, local_sem):
    me = lax.axis_index("blk")
    column = lax.axis_index("grp")
    ring = count // 2
    base = (me // ring) * ring
    half = source.shape[0] // 2
    pieces = (pl.ds(0, half), pl.ds(half, half))

    def along(step):
        return base + lax.rem(me - base + step + ring, ring)

    def across(device):
        return lax.rem(device + ring, count)

    partner, right, left, opposite = across(me), along(1), along(-1), along(2)
    local = pltpu.make_async_copy(source, gathered.at[me], local_sem)
    local.start()

    def transfer(origin, target, slot, piece=None):
        src = source if origin is me else gathered.at[origin]
        dst = gathered.at[origin]
        if piece is not None:
            src, dst = src.at[pieces[piece]], dst.at[pieces[piece]]
        return pltpu.make_async_remote_copy(
            src_ref=src,
            dst_ref=dst,
            send_sem=send_sems.at[slot],
            recv_sem=recv_sems.at[origin, 0 if piece is None else piece],
            device_id=(target, column),
            device_id_type=pl.DeviceIdType.MESH,
        )

    sent = [transfer(me, partner, 0), transfer(me, right, 1), transfer(me, left, 2)]
    for copy in sent:
        copy.start()
    relays = [
        (partner, partner, ((right, 3, None), (left, 4, None))),
        (left, left, ((right, 5, 0),)),
        (right, right, ((left, 6, 1),)),
        (across(left), left, ((right, 7, 0),)),
        (across(right), right, ((left, 8, 1),)),
    ]
    for origin, sender, onward in relays:
        transfer(origin, sender, 0).wait_recv()
        for target, slot, piece in onward:
            copy = transfer(origin, target, slot, piece)
            copy.start()
            sent.append(copy)
    for origin in (opposite, across(opposite)):
        transfer(origin, left, 0, 0).wait_recv()
        transfer(origin, right, 0, 1).wait_recv()
    for copy in sent:
        copy.wait_send()
    local.wait()


def gather_blk(piece):
    count = lax.axis_size("blk")
    rows, width = piece.shape
    return pl.pallas_call(
        functools.partial(gather_kernel, count),
        out_shape=jax.ShapeDtypeStruct((count, rows, width), piece.dtype),
        in_specs=[pl.BlockSpec(memory_space=pl.ANY)],
        out_specs=pl.BlockSpec(memory_space=pl.ANY),
        scratch_shapes=[
            pltpu.SemaphoreType.DMA((count + 1,)),
            pltpu.SemaphoreType.DMA((count, 2)),
            pltpu.SemaphoreType.DMA(()),
        ],
        compiler_params=pltpu.CompilerParams(has_side_effects=True),
        cost_estimate=pl.CostEstimate(flops=0, bytes_accessed=2 * count * rows * width * 2, transcendentals=0),
    )(piece)


def shards(amplitudes, pair_screen, integrals, tile_ab, tile_cd, residual_in):
    grp_count = lax.axis_size("grp")
    grp_position = lax.axis_index("grp")
    owner_rows, ab_tiles, tile_width = residual_in.shape
    group_rows = amplitudes.shape[1]
    row_mask = jnp.repeat(pair_screen, owner_rows, axis=1).astype(jnp.bfloat16)
    masked = amplitudes * row_mask[:, :, None]
    column_cd = lax.dynamic_index_in_dim(tile_cd, grp_position, 1, keepdims=False)
    column_ab = lax.dynamic_index_in_dim(tile_ab, grp_position, 1, keepdims=False)
    column_slot = slot_of(column_ab)
    all_slot = slot_of(tile_ab)
    slot_hit = all_slot[:, None, :] == jnp.arange(SLOTS)[None, :, None]
    ab_hit = tile_ab[None, :, :] == jnp.arange(ab_tiles)[:, None, None]
    onehot = jnp.any(ab_hit[:, :, None, :] & slot_hit[None, :, :, :], axis=1).astype(jnp.float32)
    chunk = tile_width // CHUNKS
    chunked = jnp.transpose(integrals.reshape(integrals.shape[1], CHUNKS, chunk), (1, 0, 2))
    halves = jnp.transpose(integrals.reshape(integrals.shape[1], 2, tile_width // 2), (1, 0, 2))
    offloaded = lax.all_gather(halves[0:1], "blk", axis=0, tiled=True)
    def contract(portion):
        width = portion.shape[2]
        running = jnp.zeros((SLOTS, group_rows, width), jnp.float32)
        for offset in range(portion.shape[0]):
            rows_in = lax.dynamic_index_in_dim(masked, column_cd[offset], 0, keepdims=False)
            product = jnp.dot(rows_in, portion[offset], preferred_element_type=jnp.float32)
            slot = column_slot[offset]
            earlier = lax.dynamic_index_in_dim(running, slot, 0, keepdims=False)
            running = lax.dynamic_update_index_in_dim(running, earlier + product, slot, 0)
        return running

    def exchange(running):
        width = running.shape[2]
        return lax.all_to_all(
            running.reshape(SLOTS, grp_count, owner_rows, width),
            "grp",
            split_axis=1,
            concat_axis=1,
            tiled=True,
        )

    def accumulate(arrived):
        return jnp.einsum(
            "nsg,sgrc->rnc", onehot, arrived, precision=lax.Precision.HIGHEST, preferred_element_type=jnp.float32
        )

    early_portion, ready = lax.optimization_barrier((gather_blk(chunked[CHUNKS // 2]), offloaded))
    early = exchange(contract(early_portion))
    late_sums = contract(gather_blk(chunked[CHUNKS - 1]))
    offloaded_arrived = exchange(contract(ready))
    late_sums, offloaded_arrived = lax.optimization_barrier((late_sums, offloaded_arrived))
    pieces = [accumulate(offloaded_arrived), accumulate(early), accumulate(exchange(late_sums))]
    summed = jnp.concatenate(pieces, axis=2)
    return residual_in + summed


def solution(mesh):
    in_specs = (
        P(None, "blk", None),
        P(None, "blk"),
        P(("blk", "grp"), None, None),
        P(),
        P(),
        P(("blk", "grp"), None, None),
    )
    out_specs = P(("blk", "grp"), None, None)
    return jax.shard_map(shards, mesh=mesh, in_specs=in_specs, out_specs=out_specs, check_vma=False)
```

```python
import functools

import jax
import jax.numpy as jnp
from jax import lax
from jax.experimental import pallas as pl
from jax.experimental.pallas import tpu as pltpu
from jax.sharding import PartitionSpec as P

SLOTS = 4
CHUNKS = 4


def slot_of(column_ab):
    tiles = column_ab.shape[0]
    order = jnp.arange(tiles).reshape((tiles,) + (1,) * (column_ab.ndim - 1))
    same = column_ab[:, None] == column_ab[None, :]
    first = jnp.argmax(same, axis=1)
    is_first = first == order
    earlier = order[None, :] < first[:, None]
    return jnp.sum(earlier & is_first[None, :], axis=1).astype(jnp.int32)


def gather_kernel(count, source, gathered, send_sems, recv_sems, local_sem):
    me = lax.axis_index("blk")
    column = lax.axis_index("grp")
    ring = count // 2
    base = (me // ring) * ring
    half = source.shape[0] // 2
    pieces = (pl.ds(0, half), pl.ds(half, half))

    def along(step):
        return base + lax.rem(me - base + step + ring, ring)

    def across(device):
        return lax.rem(device + ring, count)

    partner, right, left, opposite = across(me), along(1), along(-1), along(2)
    local = pltpu.make_async_copy(source, gathered.at[me], local_sem)
    local.start()

    def transfer(origin, target, slot, piece=None):
        src = source if origin is me else gathered.at[origin]
        dst = gathered.at[origin]
        if piece is not None:
            src, dst = src.at[pieces[piece]], dst.at[pieces[piece]]
        return pltpu.make_async_remote_copy(
            src_ref=src,
            dst_ref=dst,
            send_sem=send_sems.at[slot],
            recv_sem=recv_sems.at[origin, 0 if piece is None else piece],
            device_id=(target, column),
            device_id_type=pl.DeviceIdType.MESH,
        )

    sent = [transfer(me, partner, 0), transfer(me, right, 1), transfer(me, left, 2)]
    for copy in sent:
        copy.start()
    relays = [
        (partner, partner, ((right, 3, None), (left, 4, None))),
        (left, left, ((right, 5, 0),)),
        (right, right, ((left, 6, 1),)),
        (across(left), left, ((right, 7, 0),)),
        (across(right), right, ((left, 8, 1),)),
    ]
    for origin, sender, onward in relays:
        transfer(origin, sender, 0).wait_recv()
        for target, slot, piece in onward:
            copy = transfer(origin, target, slot, piece)
            copy.start()
            sent.append(copy)
    for origin in (opposite, across(opposite)):
        transfer(origin, left, 0, 0).wait_recv()
        transfer(origin, right, 0, 1).wait_recv()
    for copy in sent:
        copy.wait_send()
    local.wait()


def gather_blk(piece):
    count = lax.axis_size("blk")
    rows, width = piece.shape
    return pl.pallas_call(
        functools.partial(gather_kernel, count),
        out_shape=jax.ShapeDtypeStruct((count, rows, width), piece.dtype),
        in_specs=[pl.BlockSpec(memory_space=pl.ANY)],
        out_specs=pl.BlockSpec(memory_space=pl.ANY),
        scratch_shapes=[
            pltpu.SemaphoreType.DMA((count + 1,)),
            pltpu.SemaphoreType.DMA((count, 2)),
            pltpu.SemaphoreType.DMA(()),
        ],
        compiler_params=pltpu.CompilerParams(has_side_effects=True),
        cost_estimate=pl.CostEstimate(flops=0, bytes_accessed=2 * count * rows * width * 2, transcendentals=0),
    )(piece)


def shards(amplitudes, pair_screen, integrals, tile_ab, tile_cd, residual_in):
    grp_count = lax.axis_size("grp")
    grp_position = lax.axis_index("grp")
    owner_rows, ab_tiles, tile_width = residual_in.shape
    group_rows = amplitudes.shape[1]
    row_mask = jnp.repeat(pair_screen, owner_rows, axis=1).astype(jnp.bfloat16)
    masked = amplitudes * row_mask[:, :, None]
    column_cd = lax.dynamic_index_in_dim(tile_cd, grp_position, 1, keepdims=False)
    column_ab = lax.dynamic_index_in_dim(tile_ab, grp_position, 1, keepdims=False)
    column_slot = slot_of(column_ab)
    all_slot = slot_of(tile_ab)
    slot_hit = all_slot[:, None, :] == jnp.arange(SLOTS)[None, :, None]
    ab_hit = tile_ab[None, :, :] == jnp.arange(ab_tiles)[:, None, None]
    onehot = jnp.any(ab_hit[:, :, None, :] & slot_hit[None, :, :, :], axis=1).astype(jnp.float32)
    chunk = tile_width // CHUNKS
    chunked = jnp.transpose(integrals.reshape(integrals.shape[1], CHUNKS, chunk), (1, 0, 2))
    halves = jnp.transpose(integrals.reshape(integrals.shape[1], 2, tile_width // 2), (1, 0, 2))
    offloaded = lax.all_gather(halves[0:1], "blk", axis=0, tiled=True)
    def contract(portion):
        width = portion.shape[2]
        running = jnp.zeros((SLOTS, group_rows, width), jnp.float32)
        for offset in range(portion.shape[0]):
            rows_in = lax.dynamic_index_in_dim(masked, column_cd[offset], 0, keepdims=False)
            product = jnp.dot(rows_in, portion[offset], preferred_element_type=jnp.float32)
            slot = column_slot[offset]
            earlier = lax.dynamic_index_in_dim(running, slot, 0, keepdims=False)
            running = lax.dynamic_update_index_in_dim(running, earlier + product, slot, 0)
        return running

    def exchange(running):
        width = running.shape[2]
        return lax.all_to_all(
            running.reshape(SLOTS, grp_count, owner_rows, width),
            "grp",
            split_axis=1,
            concat_axis=1,
            tiled=True,
        )

    def accumulate(arrived):
        return jnp.einsum(
            "nsg,sgrc->rnc", onehot, arrived, precision=lax.Precision.HIGHEST, preferred_element_type=jnp.float32
        )

    early_portion, ready = lax.optimization_barrier((gather_blk(chunked[CHUNKS // 2]), offloaded))
    early_sums = contract(early_portion)
    offloaded_arrived = exchange(contract(ready))
    early_sums, offloaded_arrived = lax.optimization_barrier((early_sums, offloaded_arrived))
    early = exchange(early_sums)
    late_sums = contract(gather_blk(chunked[CHUNKS - 1]))
    pieces = [accumulate(offloaded_arrived), accumulate(early), accumulate(exchange(late_sums))]
    summed = jnp.concatenate(pieces, axis=2)
    return residual_in + summed


def solution(mesh):
    in_specs = (
        P(None, "blk", None),
        P(None, "blk"),
        P(("blk", "grp"), None, None),
        P(),
        P(),
        P(("blk", "grp"), None, None),
    )
    out_specs = P(("blk", "grp"), None, None)
    return jax.shard_map(shards, mesh=mesh, in_specs=in_specs, out_specs=out_specs, check_vma=False)
```

```python
import functools

import jax
import jax.numpy as jnp
from jax import lax
from jax.experimental import pallas as pl
from jax.experimental.pallas import tpu as pltpu
from jax.sharding import PartitionSpec as P

SLOTS = 4
CHUNKS = 4


def slot_of(column_ab):
    tiles = column_ab.shape[0]
    order = jnp.arange(tiles).reshape((tiles,) + (1,) * (column_ab.ndim - 1))
    same = column_ab[:, None] == column_ab[None, :]
    first = jnp.argmax(same, axis=1)
    is_first = first == order
    earlier = order[None, :] < first[:, None]
    return jnp.sum(earlier & is_first[None, :], axis=1).astype(jnp.int32)


def gather_kernel(count, source, gathered, send_sems, recv_sems, local_sem):
    me = lax.axis_index("blk")
    column = lax.axis_index("grp")
    ring = count // 2
    base = (me // ring) * ring
    half = source.shape[0] // 2
    pieces = (pl.ds(0, half), pl.ds(half, half))

    def along(step):
        return base + lax.rem(me - base + step + ring, ring)

    def across(device):
        return lax.rem(device + ring, count)

    partner, right, left, opposite = across(me), along(1), along(-1), along(2)
    local = pltpu.make_async_copy(source, gathered.at[me], local_sem)
    local.start()

    def transfer(origin, target, slot, piece=None):
        src = source if origin is me else gathered.at[origin]
        dst = gathered.at[origin]
        if piece is not None:
            src, dst = src.at[pieces[piece]], dst.at[pieces[piece]]
        return pltpu.make_async_remote_copy(
            src_ref=src,
            dst_ref=dst,
            send_sem=send_sems.at[slot],
            recv_sem=recv_sems.at[origin, 0 if piece is None else piece],
            device_id=(target, column),
            device_id_type=pl.DeviceIdType.MESH,
        )

    sent = [transfer(me, partner, 0), transfer(me, right, 1), transfer(me, left, 2)]
    for copy in sent:
        copy.start()
    relays = [
        (partner, partner, ((right, 3, None), (left, 4, None))),
        (left, left, ((right, 5, 0),)),
        (right, right, ((left, 6, 1),)),
        (across(left), left, ((right, 7, 0),)),
        (across(right), right, ((left, 8, 1),)),
    ]
    for origin, sender, onward in relays:
        transfer(origin, sender, 0).wait_recv()
        for target, slot, piece in onward:
            copy = transfer(origin, target, slot, piece)
            copy.start()
            sent.append(copy)
    for origin in (opposite, across(opposite)):
        transfer(origin, left, 0, 0).wait_recv()
        transfer(origin, right, 0, 1).wait_recv()
    for copy in sent:
        copy.wait_send()
    local.wait()


def gather_blk(piece):
    count = lax.axis_size("blk")
    rows, width = piece.shape
    return pl.pallas_call(
        functools.partial(gather_kernel, count),
        out_shape=jax.ShapeDtypeStruct((count, rows, width), piece.dtype),
        in_specs=[pl.BlockSpec(memory_space=pl.ANY)],
        out_specs=pl.BlockSpec(memory_space=pl.ANY),
        scratch_shapes=[
            pltpu.SemaphoreType.DMA((count + 1,)),
            pltpu.SemaphoreType.DMA((count, 2)),
            pltpu.SemaphoreType.DMA(()),
        ],
        compiler_params=pltpu.CompilerParams(has_side_effects=True),
        cost_estimate=pl.CostEstimate(flops=0, bytes_accessed=2 * count * rows * width * 2, transcendentals=0),
    )(piece)


def shards(amplitudes, pair_screen, integrals, tile_ab, tile_cd, residual_in):
    grp_count = lax.axis_size("grp")
    grp_position = lax.axis_index("grp")
    owner_rows, ab_tiles, tile_width = residual_in.shape
    group_rows = amplitudes.shape[1]
    row_mask = jnp.repeat(pair_screen, owner_rows, axis=1).astype(jnp.bfloat16)
    masked = amplitudes * row_mask[:, :, None]
    column_cd = lax.dynamic_index_in_dim(tile_cd, grp_position, 1, keepdims=False)
    column_ab = lax.dynamic_index_in_dim(tile_ab, grp_position, 1, keepdims=False)
    column_slot = slot_of(column_ab)
    all_slot = slot_of(tile_ab)
    slot_hit = all_slot[:, None, :] == jnp.arange(SLOTS)[None, :, None]
    ab_hit = tile_ab[None, :, :] == jnp.arange(ab_tiles)[:, None, None]
    onehot = jnp.any(ab_hit[:, :, None, :] & slot_hit[None, :, :, :], axis=1).astype(jnp.float32)
    chunk = tile_width // CHUNKS
    chunked = jnp.transpose(integrals.reshape(integrals.shape[1], CHUNKS, chunk), (1, 0, 2))
    halves = jnp.transpose(integrals.reshape(integrals.shape[1], 2, tile_width // 2), (1, 0, 2))
    offloaded = lax.all_gather(halves[0:1], "blk", axis=0, tiled=True)
    def contract(portion):
        width = portion.shape[2]
        running = jnp.zeros((SLOTS, group_rows, width), jnp.float32)
        for offset in range(portion.shape[0]):
            rows_in = lax.dynamic_index_in_dim(masked, column_cd[offset], 0, keepdims=False)
            product = jnp.dot(rows_in, portion[offset], preferred_element_type=jnp.float32)
            slot = column_slot[offset]
            earlier = lax.dynamic_index_in_dim(running, slot, 0, keepdims=False)
            running = lax.dynamic_update_index_in_dim(running, earlier + product, slot, 0)
        return running

    def exchange(running):
        width = running.shape[2]
        return lax.all_to_all(
            running.reshape(SLOTS, grp_count, owner_rows, width),
            "grp",
            split_axis=1,
            concat_axis=1,
            tiled=True,
        )

    def accumulate(arrived):
        return jnp.einsum(
            "nsg,sgrc->rnc", onehot, arrived, precision=lax.Precision.HIGHEST, preferred_element_type=jnp.float32
        )

    early_portion, ready = lax.optimization_barrier((gather_blk(chunked[CHUNKS // 2]), offloaded))
    early_sums = contract(early_portion)
    offloaded_arrived = exchange(contract(ready))
    early_sums, offloaded_arrived = lax.optimization_barrier((early_sums, offloaded_arrived))
    late_sums = contract(gather_blk(chunked[CHUNKS - 1]))
    pieces = [accumulate(offloaded_arrived), accumulate(exchange(jnp.concatenate([early_sums, late_sums], axis=2)))]
    summed = jnp.concatenate(pieces, axis=2)
    return residual_in + summed


def solution(mesh):
    in_specs = (
        P(None, "blk", None),
        P(None, "blk"),
        P(("blk", "grp"), None, None),
        P(),
        P(),
        P(("blk", "grp"), None, None),
    )
    out_specs = P(("blk", "grp"), None, None)
    return jax.shard_map(shards, mesh=mesh, in_specs=in_specs, out_specs=out_specs, check_vma=False)
```
